32 devices in a mesh: space: 16 (over z, y, core), chan: 2 (over x).
Axes of the slice: x: 2, y: 2, z: 4, core: 2. Of those that a mesh axis runs over, the one named last changes fastest.
Arguments:
- volume: bfloat16 [8, 32, 128, 256], P(None, 'space', None, 'chan'), may hold values from -6 to 6
- first_filter: bfloat16 [3, 3, 3, 256, 256], P(None, None, None, None, 'chan'), may hold values from -0.078125 to 0.078125
- second_filter: bfloat16 [3, 3, 3, 256, 256], P(None, None, None, None, 'chan'), may hold values from -0.078125 to 0.078125
Outputs:
- block_out: bfloat16 [8, 32, 128, 256], P(None, 'space', None, 'chan')
The draws below stay inside these ranges and needn't reach their ends.
All inputs are finite; a program needn't handle non-finite values.
Results may differ from the reference program's by a relative error of at most 0.0032.
Values may be sent and summed in bfloat16 or wider, within the bound.
A program may use at most 128 MiB of HBM per device.

```python
import jax
import jax.numpy as jnp
from jax import lax

C = 256
DEPTH = 8
WIDTH = 128
HEIGHT = 32


def block_levels(stream_key, dims, cuts, low, largest):
    level = 1.0
    for axis_at, blocks in cuts:
        steps = jax.random.uniform(jax.random.fold_in(jax.random.fold_in(stream_key, 6), axis_at), (blocks,), jnp.float32, low / len(cuts), largest / len(cuts))
        level = level * jnp.repeat(jnp.exp(steps), dims[axis_at] // blocks).reshape((-1,) + (1,) * (len(dims) - 1 - axis_at))
    return level


def centred(own_key, extent, spread, reach, shards=(), kind=jnp.bfloat16):
    values = spread * jax.random.normal(own_key, extent, jnp.float32)
    if shards:
        values = values * block_levels(own_key, extent, shards, -0.22, 0.18)
    return jnp.clip(values, -reach, reach).astype(kind)


def setup_inputs(seed: int = 0) -> dict:
    key_list = jax.random.split(jax.random.key(seed), 4)
    return {
        "volume": centred(key_list[0], (DEPTH, HEIGHT, WIDTH, C), 1.0, 6.0, ((1, 16), (3, 2))),
        "first_filter": centred(key_list[1], (3, 3, 3, C, C), (27 * C) ** -0.5, 0.078125, ((4, 2),)),
        "second_filter": centred(key_list[2], (3, 3, 3, C, C), (27 * C) ** -0.5, 0.078125, ((4, 2),)),
    }


def conv(field, filt):
    out = lax.conv_general_dilated(field.astype(jnp.float32)[None], filt.astype(jnp.float32), (1, 1, 1), [(1, 1), (1, 1), (1, 1)], dimension_numbers=("NDHWC", "DHWIO", "NDHWC"), precision=lax.Precision.HIGHEST)
    return out[0]


def reference(volume, first_filter, second_filter):
    hidden = jnp.maximum(conv(volume, first_filter), 0.0).astype(jnp.bfloat16)
    total = volume.astype(jnp.float32) + conv(hidden, second_filter)
    return jnp.maximum(total, 0.0).astype(jnp.bfloat16)
```

```python
import functools

import jax
import jax.numpy as jnp
from jax import lax
from jax.experimental import pallas as pl
from jax.experimental.pallas import tpu as pltpu
from jax.sharding import PartitionSpec as P

MESH = pl.DeviceIdType.MESH
CHAN, OWN_UP, OWN_DOWN, FWD_UP, FWD_DOWN = range(5)


def shifted_out(partial, out_c):
    width = partial.shape[0]
    at = lax.broadcasted_iota(jnp.int32, (width, out_c), 0)
    left = pltpu.roll(partial[:, :out_c], 1, 0)
    right = pltpu.roll(partial[:, 2 * out_c :], width - 1, 0)
    left = jnp.where(at == 0, 0.0, left)
    right = jnp.where(at == width - 1, 0.0, right)
    return left + partial[:, out_c : 2 * out_c] + right


def kernel(
    n_space, volume, first, second, out,
    field, hidden, w1, w2, local_sem, send_sem, recv_sem,
):
    s, c = lax.axis_index("space"), lax.axis_index("chan")
    other = 1 - c
    depth, planes, width, half = volume.shape
    out_c = first.shape[4]
    has_up, has_down = s < n_space - 1, s > 0
    up, down, across = {"space": s + 1}, {"space": s - 1}, {"chan": other}

    own_copy = pltpu.make_async_copy(
        volume, field.at[c, pl.ds(1, depth), pl.ds(1, planes)], local_sem.at[0]
    )
    own_copy.start()
    filter_copies = []
    for k, (src, dst) in enumerate(((first, w1), (second, w2))):
        for tap in range(3):
            filter_copies.append(
                pltpu.make_async_copy(
                    src.at[:, :, tap],
                    dst.at[:, :, :, pl.ds(tap * out_c, out_c)],
                    local_sem.at[1 + 3 * k + tap],
                )
            )
    for copy in filter_copies:
        copy.start()

    barrier = pltpu.get_barrier_semaphore()
    pl.semaphore_signal(barrier, inc=1, device_id=across, device_id_type=MESH)

    @pl.when(has_up)
    def _():
        pl.semaphore_signal(barrier, inc=1, device_id=up, device_id_type=MESH)

    @pl.when(has_down)
    def _():
        pl.semaphore_signal(barrier, inc=1, device_id=down, device_id_type=MESH)

    line = jnp.zeros((planes + 2, width, half), field.dtype)
    for buf in (field, hidden):
        for h in range(2):
            buf[h, 0] = line
            buf[h, depth + 1] = line

    @pl.when(jnp.logical_not(has_down))
    def _():
        for buf in (field, hidden):
            for h in range(2):
                buf[h, :, 0] = jnp.zeros((depth + 2, width, half), field.dtype)

    @pl.when(jnp.logical_not(has_up))
    def _():
        for buf in (field, hidden):
            for h in range(2):
                buf[h, :, planes + 1] = jnp.zeros((depth + 2, width, half), field.dtype)

    pl.semaphore_wait(barrier, 1 + has_up.astype(jnp.int32) + has_down.astype(jnp.int32))

    def remote(phase, kind, d, own_src=None):
        buf = field if phase == 0 else hidden
        which = other if kind in (FWD_UP, FWD_DOWN) else c
        if kind == CHAN:
            src, dst, dev = pl.ds(1, planes), pl.ds(1, planes), across
        elif kind in (OWN_UP, FWD_UP):
            src, dst, dev = pl.ds(planes, 1), pl.ds(0, 1), up
        else:
            src, dst, dev = pl.ds(1, 1), pl.ds(planes + 1, 1), down
        source = buf.at[which, d + 1, src]
        return pltpu.make_async_remote_copy(
            src_ref=source,
            dst_ref=buf.at[which, d + 1, dst],
            send_sem=send_sem.at[phase, kind, d],
            recv_sem=recv_sem.at[phase, kind, d],
            device_id=dev,
            device_id_type=MESH,
        )

    def send_own(phase, d):
        remote(phase, CHAN, d).start()

        @pl.when(has_up)
        def _():
            remote(phase, OWN_UP, d).start()

        @pl.when(has_down)
        def _():
            remote(phase, OWN_DOWN, d).start()

    def forward(phase, d):
        remote(phase, CHAN, d).wait_recv()

        @pl.when(has_up)
        def _():
            remote(phase, FWD_UP, d).start()

        @pl.when(has_down)
        def _():
            remote(phase, FWD_DOWN, d).start()

    def await_halo(phase, d):
        @pl.when(has_down)
        def _():
            remote(phase, OWN_UP, d).wait_recv()
            remote(phase, FWD_UP, d).wait_recv()

        @pl.when(has_up)
        def _():
            remote(phase, OWN_DOWN, d).wait_recv()
            remote(phase, FWD_DOWN, d).wait_recv()

    def conv(buf, w, d):
        pieces = [
            buf[h, d + a, b : b + planes].reshape(planes * width, half)
            for a in range(3)
            for b in range(3)
            for h in range(2)
        ]
        lhs = jnp.concatenate(pieces, axis=1)
        partial = jnp.dot(
            lhs, w[...].reshape(lhs.shape[1], 3 * out_c), preferred_element_type=jnp.float32
        )
        return [shifted_out(partial[p * width : (p + 1) * width], out_c) for p in range(planes)]

    own_copy.wait()

    def send_volume(d, carry):
        send_own(0, d)
        return carry

    lax.fori_loop(0, depth, send_volume, 0)
    for copy in filter_copies[:3]:
        copy.wait()

    def conv_phase(phase, finish):
        def step(t, carry):
            @pl.when(t < depth)
            def _():
                forward(phase, t)

            @pl.when(jnp.logical_and(t >= 1, t <= depth))
            def _():
                await_halo(phase, t - 1)

            @pl.when(t >= 2)
            def _():
                finish(t - 2)

            return carry

        lax.fori_loop(0, depth + 2, step, 0)

    def finish_hidden(d):
        for p, total in enumerate(conv(field, w1, d)):
            hidden[c, d + 1, p + 1] = jnp.maximum(total, 0.0).astype(hidden.dtype)
        send_own(1, d)

    def finish_out(d):
        for p, total in enumerate(conv(hidden, w2, d)):
            total = total + field[c, d + 1, p + 1].astype(jnp.float32)
            out[d, p] = jnp.maximum(total, 0.0).astype(out.dtype)

    conv_phase(0, finish_hidden)
    for copy in filter_copies[3:]:
        copy.wait()
    conv_phase(1, finish_out)

    def drain(d, carry):
        for phase in range(2):
            remote(phase, CHAN, d).wait_send()

            @pl.when(has_up)
            def _():
                remote(phase, OWN_UP, d).wait_send()
                remote(phase, FWD_UP, d).wait_send()

            @pl.when(has_down)
            def _():
                remote(phase, OWN_DOWN, d).wait_send()
                remote(phase, FWD_DOWN, d).wait_send()

        return carry

    lax.fori_loop(0, depth, drain, 0)


def per_device(n_space, volume, first_filter, second_filter):
    depth, planes, width, half = volume.shape
    taps_d, taps_h, taps_w, in_c, out_c = first_filter.shape
    plane_buf = pltpu.VMEM((2, depth + 2, planes + 2, width, half), jnp.bfloat16)
    filter_buf = pltpu.VMEM((taps_d, taps_h, in_c, taps_w * out_c), jnp.bfloat16)
    flops = 2 * 2 * 27 * depth * planes * width * in_c * out_c
    return pl.pallas_call(
        functools.partial(kernel, n_space),
        out_shape=jax.ShapeDtypeStruct(volume.shape, jnp.bfloat16),
        in_specs=[pl.BlockSpec(memory_space=pltpu.HBM)] * 3,
        out_specs=pl.BlockSpec(memory_space=pltpu.VMEM),
        scratch_shapes=[
            plane_buf,
            plane_buf,
            filter_buf,
            filter_buf,
            pltpu.SemaphoreType.DMA((7,)),
            pltpu.SemaphoreType.DMA((2, 5, depth)),
            pltpu.SemaphoreType.DMA((2, 5, depth)),
        ],
        compiler_params=pltpu.CompilerParams(
            collective_id=0, has_side_effects=True, vmem_limit_bytes=40 << 20
        ),
        cost_estimate=pl.CostEstimate(
            flops=flops, bytes_accessed=4 * volume.size + 4 * first_filter.size, transcendentals=0
        ),
    )(volume, first_filter, second_filter)


def solution(mesh):
    return jax.shard_map(
        functools.partial(per_device, mesh.shape["space"]),
        mesh=mesh,
        in_specs=(
            P(None, "space", None, "chan"),
            P(None, None, None, None, "chan"),
            P(None, None, None, None, "chan"),
        ),
        out_specs=P(None, "space", None, "chan"),
        check_vma=False,
    )
```

```python
import functools

import jax
import jax.numpy as jnp
from jax import lax
from jax.experimental import pallas as pl
from jax.experimental.pallas import tpu as pltpu
from jax.sharding import PartitionSpec as P

MESH = pl.DeviceIdType.MESH
LEADS = (4, 4)
CHAN, OWN_UP, OWN_DOWN, FWD_UP, FWD_DOWN = range(5)


def shifted_out(partial, out_c):
    width = partial.shape[0]
    at = lax.broadcasted_iota(jnp.int32, (width, out_c), 0)
    left = pltpu.roll(partial[:, :out_c], 1, 0)
    right = pltpu.roll(partial[:, 2 * out_c :], width - 1, 0)
    left = jnp.where(at == 0, 0.0, left)
    right = jnp.where(at == width - 1, 0.0, right)
    return left + partial[:, out_c : 2 * out_c] + right


def kernel(
    n_space, volume, first, second, out,
    field, hidden, w1, w2, local_sem, send_sem, recv_sem,
):
    s, c = lax.axis_index("space"), lax.axis_index("chan")
    other = 1 - c
    depth, planes, width, half = volume.shape
    out_c = first.shape[4]
    has_up, has_down = s < n_space - 1, s > 0
    up, down, across = {"space": s + 1}, {"space": s - 1}, {"chan": other}

    own_copy = pltpu.make_async_copy(
        volume, field.at[c, pl.ds(1, depth), pl.ds(1, planes)], local_sem.at[0]
    )
    own_copy.start()
    filter_copies = []
    for k, (src, dst) in enumerate(((first, w1), (second, w2))):
        for tap in range(3):
            filter_copies.append(
                pltpu.make_async_copy(
                    src.at[:, :, tap],
                    dst.at[:, :, :, pl.ds(tap * out_c, out_c)],
                    local_sem.at[1 + 3 * k + tap],
                )
            )
    for copy in filter_copies:
        copy.start()

    barrier = pltpu.get_barrier_semaphore()
    pl.semaphore_signal(barrier, inc=1, device_id=across, device_id_type=MESH)

    @pl.when(has_up)
    def _():
        pl.semaphore_signal(barrier, inc=1, device_id=up, device_id_type=MESH)

    @pl.when(has_down)
    def _():
        pl.semaphore_signal(barrier, inc=1, device_id=down, device_id_type=MESH)

    line = jnp.zeros((planes + 2, width, half), field.dtype)
    for buf in (field, hidden):
        for h in range(2):
            buf[h, 0] = line
            buf[h, depth + 1] = line

    @pl.when(jnp.logical_not(has_down))
    def _():
        for buf in (field, hidden):
            for h in range(2):
                buf[h, :, 0] = jnp.zeros((depth + 2, width, half), field.dtype)

    @pl.when(jnp.logical_not(has_up))
    def _():
        for buf in (field, hidden):
            for h in range(2):
                buf[h, :, planes + 1] = jnp.zeros((depth + 2, width, half), field.dtype)

    pl.semaphore_wait(barrier, 1 + has_up.astype(jnp.int32) + has_down.astype(jnp.int32))

    def remote(phase, kind, d):
        buf = field if phase == 0 else hidden
        which = other if kind in (FWD_UP, FWD_DOWN) else c
        if kind == CHAN:
            src, dst, dev = pl.ds(1, planes), pl.ds(1, planes), across
        elif kind in (OWN_UP, FWD_UP):
            src, dst, dev = pl.ds(planes, 1), pl.ds(0, 1), up
        else:
            src, dst, dev = pl.ds(1, 1), pl.ds(planes + 1, 1), down
        if phase == 0 and kind == CHAN:
            source = volume.at[d]
        elif phase == 0 and kind == OWN_UP:
            source = volume.at[d, pl.ds(planes - 1, 1)]
        elif phase == 0 and kind == OWN_DOWN:
            source = volume.at[d, pl.ds(0, 1)]
        else:
            source = buf.at[which, d + 1, src]
        return pltpu.make_async_remote_copy(
            src_ref=source,
            dst_ref=buf.at[which, d + 1, dst],
            send_sem=send_sem.at[phase, kind, d],
            recv_sem=recv_sem.at[phase, kind, d],
            device_id=dev,
            device_id_type=MESH,
        )

    def send_own(phase, d):
        remote(phase, CHAN, d).start()

        @pl.when(has_up)
        def _():
            remote(phase, OWN_UP, d).start()

        @pl.when(has_down)
        def _():
            remote(phase, OWN_DOWN, d).start()

    def forward(phase, d):
        remote(phase, CHAN, d).wait_recv()

        @pl.when(has_up)
        def _():
            remote(phase, FWD_UP, d).start()

        @pl.when(has_down)
        def _():
            remote(phase, FWD_DOWN, d).start()

    def await_halo(phase, d):
        @pl.when(has_down)
        def _():
            remote(phase, OWN_UP, d).wait_recv()
            remote(phase, FWD_UP, d).wait_recv()

        @pl.when(has_up)
        def _():
            remote(phase, OWN_DOWN, d).wait_recv()
            remote(phase, FWD_DOWN, d).wait_recv()

    def conv(buf, w, d):
        pieces = [
            buf[h, d + a, b : b + planes].reshape(planes * width, half)
            for a in range(3)
            for b in range(3)
            for h in range(2)
        ]
        lhs = jnp.concatenate(pieces, axis=1)
        partial = jnp.dot(
            lhs, w[...].reshape(lhs.shape[1], 3 * out_c), preferred_element_type=jnp.float32
        )
        return [shifted_out(partial[p * width : (p + 1) * width], out_c) for p in range(planes)]

    def send_volume(d, carry):
        send_own(0, d)
        return carry

    lax.fori_loop(0, depth, send_volume, 0)
    own_copy.wait()
    for copy in filter_copies[:3]:
        copy.wait()

    def conv_phase(phase, lead, finish):
        def step(t, carry):
            @pl.when(t < depth)
            def _():
                forward(phase, t)

            @pl.when(jnp.logical_and(t >= lead - 1, t < lead - 1 + depth))
            def _():
                await_halo(phase, t - (lead - 1))

            @pl.when(t >= lead)
            def _():
                finish(t - lead)

            return carry

        lax.fori_loop(0, depth + lead, step, 0)

    def finish_hidden(d):
        for p, total in enumerate(conv(field, w1, d)):
            hidden[c, d + 1, p + 1] = jnp.maximum(total, 0.0).astype(hidden.dtype)
        send_own(1, d)

    def finish_out(d):
        for p, total in enumerate(conv(hidden, w2, d)):
            total = total + field[c, d + 1, p + 1].astype(jnp.float32)
            out[d, p] = jnp.maximum(total, 0.0).astype(out.dtype)

    conv_phase(0, LEADS[0], finish_hidden)
    for copy in filter_copies[3:]:
        copy.wait()
    conv_phase(1, LEADS[1], finish_out)

    def drain(d, carry):
        for phase in range(2):
            remote(phase, CHAN, d).wait_send()

            @pl.when(has_up)
            def _():
                remote(phase, OWN_UP, d).wait_send()
                remote(phase, FWD_UP, d).wait_send()

            @pl.when(has_down)
            def _():
                remote(phase, OWN_DOWN, d).wait_send()
                remote(phase, FWD_DOWN, d).wait_send()

        return carry

    lax.fori_loop(0, depth, drain, 0)


def per_device(n_space, volume, first_filter, second_filter):
    depth, planes, width, half = volume.shape
    taps_d, taps_h, taps_w, in_c, out_c = first_filter.shape
    plane_buf = pltpu.VMEM((2, depth + 2, planes + 2, width, half), jnp.bfloat16)
    filter_buf = pltpu.VMEM((taps_d, taps_h, in_c, taps_w * out_c), jnp.bfloat16)
    flops = 2 * 2 * 27 * depth * planes * width * in_c * out_c
    return pl.pallas_call(
        functools.partial(kernel, n_space),
        out_shape=jax.ShapeDtypeStruct(volume.shape, jnp.bfloat16),
        in_specs=[pl.BlockSpec(memory_space=pltpu.HBM)] * 3,
        out_specs=pl.BlockSpec(memory_space=pltpu.VMEM),
        scratch_shapes=[
            plane_buf,
            plane_buf,
            filter_buf,
            filter_buf,
            pltpu.SemaphoreType.DMA((7,)),
            pltpu.SemaphoreType.DMA((2, 5, depth)),
            pltpu.SemaphoreType.DMA((2, 5, depth)),
        ],
        compiler_params=pltpu.CompilerParams(
            collective_id=0, has_side_effects=True, vmem_limit_bytes=60 << 20
        ),
        cost_estimate=pl.CostEstimate(
            flops=flops, bytes_accessed=4 * volume.size + 4 * first_filter.size, transcendentals=0
        ),
    )(volume, first_filter, second_filter)


def solution(mesh):
    return jax.shard_map(
        functools.partial(per_device, mesh.shape["space"]),
        mesh=mesh,
        in_specs=(
            P(None, "space", None, "chan"),
            P(None, None, None, None, "chan"),
            P(None, None, None, None, "chan"),
        ),
        out_specs=P(None, "space", None, "chan"),
        check_vma=False,
    )
```

```python
import functools

import jax
import jax.numpy as jnp
from jax import lax
from jax.experimental import pallas as pl
from jax.experimental.pallas import tpu as pltpu
from jax.sharding import PartitionSpec as P

MESH = pl.DeviceIdType.MESH
LEADS = (4, 4)
CHAN, OWN_UP, OWN_DOWN, FWD_UP, FWD_DOWN = range(5)


def shifted_out(partial, out_c):
    width = partial.shape[0]
    at = lax.broadcasted_iota(jnp.int32, (width, out_c), 0)
    left = pltpu.roll(partial[:, :out_c], 1, 0)
    right = pltpu.roll(partial[:, 2 * out_c :], width - 1, 0)
    left = jnp.where(at == 0, 0.0, left)
    right = jnp.where(at == width - 1, 0.0, right)
    return left + partial[:, out_c : 2 * out_c] + right


def kernel(
    n_space, volume, first, second, out,
    field, hidden, w1, w2, local_sem, send_sem, recv_sem,
):
    s, c = lax.axis_index("space"), lax.axis_index("chan")
    other = 1 - c
    depth, planes, width, half = volume.shape
    out_c = first.shape[4]
    has_up, has_down = s < n_space - 1, s > 0
    up, down, across = {"space": s + 1}, {"space": s - 1}, {"chan": other}

    own_copy = pltpu.make_async_copy(
        volume, field.at[c, pl.ds(1, depth), pl.ds(1, planes)], local_sem.at[0]
    )
    own_copy.start()
    filter_copies = []
    for k, (src, dst) in enumerate(((first, w1), (second, w2))):
        for tap in range(3):
            filter_copies.append(
                pltpu.make_async_copy(
                    src.at[:, :, tap],
                    dst.at[:, :, :, pl.ds(tap * out_c, out_c)],
                    local_sem.at[1 + 3 * k + tap],
                )
            )
    for copy in filter_copies:
        copy.start()

    barrier = pltpu.get_barrier_semaphore()
    pl.semaphore_signal(barrier, inc=1, device_id=across, device_id_type=MESH)

    @pl.when(has_up)
    def _():
        pl.semaphore_signal(barrier, inc=1, device_id=up, device_id_type=MESH)

    @pl.when(has_down)
    def _():
        pl.semaphore_signal(barrier, inc=1, device_id=down, device_id_type=MESH)

    line = jnp.zeros((planes + 2, width, half), field.dtype)
    for buf in (field, hidden):
        for h in range(2):
            buf[h, 0] = line
            buf[h, depth + 1] = line

    @pl.when(jnp.logical_not(has_down))
    def _():
        for buf in (field, hidden):
            for h in range(2):
                buf[h, :, 0] = jnp.zeros((depth + 2, width, half), field.dtype)

    @pl.when(jnp.logical_not(has_up))
    def _():
        for buf in (field, hidden):
            for h in range(2):
                buf[h, :, planes + 1] = jnp.zeros((depth + 2, width, half), field.dtype)

    pl.semaphore_wait(barrier, 1 + has_up.astype(jnp.int32) + has_down.astype(jnp.int32))

    def remote(phase, kind, d):
        buf = field if phase == 0 else hidden
        which = other if kind in (FWD_UP, FWD_DOWN) else c
        if kind == CHAN:
            src, dst, dev = pl.ds(1, planes), pl.ds(1, planes), across
        elif kind in (OWN_UP, FWD_UP):
            src, dst, dev = pl.ds(planes, 1), pl.ds(0, 1), up
        else:
            src, dst, dev = pl.ds(1, 1), pl.ds(planes + 1, 1), down
        if phase == 0 and kind == CHAN:
            source = volume.at[d]
        elif phase == 0 and kind == OWN_UP:
            source = volume.at[d, pl.ds(planes - 1, 1)]
        elif phase == 0 and kind == OWN_DOWN:
            source = volume.at[d, pl.ds(0, 1)]
        else:
            source = buf.at[which, d + 1, src]
        return pltpu.make_async_remote_copy(
            src_ref=source,
            dst_ref=buf.at[which, d + 1, dst],
            send_sem=send_sem.at[phase, kind, d],
            recv_sem=recv_sem.at[phase, kind, d],
            device_id=dev,
            device_id_type=MESH,
        )

    def send_own(phase, d):
        remote(phase, CHAN, d).start()

        @pl.when(has_up)
        def _():
            remote(phase, OWN_UP, d).start()

        @pl.when(has_down)
        def _():
            remote(phase, OWN_DOWN, d).start()

    def forward(phase, d):
        remote(phase, CHAN, d).wait_recv()

        @pl.when(has_up)
        def _():
            remote(phase, FWD_UP, d).start()

        @pl.when(has_down)
        def _():
            remote(phase, FWD_DOWN, d).start()

    def await_halo(phase, d):
        @pl.when(has_down)
        def _():
            remote(phase, OWN_UP, d).wait_recv()
            remote(phase, FWD_UP, d).wait_recv()

        @pl.when(has_up)
        def _():
            remote(phase, OWN_DOWN, d).wait_recv()
            remote(phase, FWD_DOWN, d).wait_recv()

    def conv(buf, w, d):
        pieces = [
            buf[h, d + a, b : b + planes].reshape(planes * width, half)
            for a in range(3)
            for b in range(3)
            for h in range(2)
        ]
        lhs = jnp.concatenate(pieces, axis=1)
        partial = jnp.dot(
            lhs, w[...].reshape(lhs.shape[1], 3 * out_c), preferred_element_type=jnp.float32
        )
        return [shifted_out(partial[p * width : (p + 1) * width], out_c) for p in range(planes)]

    def send_volume(d, carry):
        send_own(0, d)
        return carry

    lax.fori_loop(0, depth, send_volume, 0)
    own_copy.wait()
    for copy in filter_copies[:3]:
        copy.wait()

    def conv_phase(phase, lead, finish):
        def step(t, carry):
            @pl.when(t < depth)
            def _():
                forward(phase, t)

            @pl.when(jnp.logical_and(t >= lead - 1, t < lead - 1 + depth))
            def _():
                await_halo(phase, t - (lead - 1))

            @pl.when(t >= lead)
            def _():
                finish(t - lead)

            return carry

        lax.fori_loop(0, depth + lead, step, 0)

    def finish_hidden(d):
        for p, total in enumerate(conv(field, w1, d)):
            hidden[c, d + 1, p + 1] = jnp.maximum(total, 0.0).astype(hidden.dtype)
        send_own(1, d)

    def finish_out(d):
        for p, total in enumerate(conv(hidden, w2, d)):
            total = total + field[c, d + 1, p + 1].astype(jnp.float32)
            out[d, p] = jnp.maximum(total, 0.0).astype(out.dtype)

    conv_phase(0, LEADS[0], finish_hidden)
    for copy in filter_copies[3:]:
        copy.wait()
    conv_phase(1, LEADS[1], finish_out)

    def drain(d, carry):
        for phase in range(2):
            remote(phase, CHAN, d).wait_send()

            @pl.when(has_up)
            def _():
                remote(phase, OWN_UP, d).wait_send()
                remote(phase, FWD_UP, d).wait_send()

            @pl.when(has_down)
            def _():
                remote(phase, OWN_DOWN, d).wait_send()
                remote(phase, FWD_DOWN, d).wait_send()

        return carry

    lax.fori_loop(0, depth, drain, 0)


def per_device(n_space, volume, first_filter, second_filter):
    depth, planes, width, half = volume.shape
    taps_d, taps_h, taps_w, in_c, out_c = first_filter.shape
    plane_buf = pltpu.VMEM((2, depth + 2, planes + 2, width, half), jnp.bfloat16)
    filter_buf = pltpu.VMEM((taps_d, taps_h, in_c, taps_w * out_c), jnp.bfloat16)
    flops = 2 * 2 * 27 * depth * planes * width * in_c * out_c
    volume, first_filter, second_filter = (
        pltpu.with_memory_space_constraint(x, pltpu.HBM) for x in (volume, first_filter, second_filter)
    )
    return pl.pallas_call(
        functools.partial(kernel, n_space),
        out_shape=pltpu.VMEM(volume.shape, jnp.bfloat16),
        in_specs=[pl.BlockSpec(memory_space=pltpu.HBM)] * 3,
        out_specs=pl.BlockSpec(memory_space=pltpu.VMEM),
        scratch_shapes=[
            plane_buf,
            plane_buf,
            filter_buf,
            filter_buf,
            pltpu.SemaphoreType.DMA((7,)),
            pltpu.SemaphoreType.DMA((2, 5, depth)),
            pltpu.SemaphoreType.DMA((2, 5, depth)),
        ],
        compiler_params=pltpu.CompilerParams(
            collective_id=0, has_side_effects=True, vmem_limit_bytes=32 << 20
        ),
        cost_estimate=pl.CostEstimate(
            flops=flops, bytes_accessed=4 * volume.size + 4 * first_filter.size, transcendentals=0
        ),
    )(volume, first_filter, second_filter)


def solution(mesh):
    return jax.shard_map(
        functools.partial(per_device, mesh.shape["space"]),
        mesh=mesh,
        in_specs=(
            P(None, "space", None, "chan"),
            P(None, None, None, None, "chan"),
            P(None, None, None, None, "chan"),
        ),
        out_specs=P(None, "space", None, "chan"),
        check_vma=False,
    )
```

```python
import functools

import jax
import jax.numpy as jnp
from jax import lax
from jax.experimental import pallas as pl
from jax.experimental.pallas import tpu as pltpu
from jax.sharding import PartitionSpec as P

MESH = pl.DeviceIdType.MESH
LEADS = (4, 5)
CHAN, OWN_UP, OWN_DOWN, FWD_UP, FWD_DOWN = range(5)


def shifted_out(partial, out_c):
    width = partial.shape[0]
    at = lax.broadcasted_iota(jnp.int32, (width, out_c), 0)
    left = pltpu.roll(partial[:, :out_c], 1, 0)
    right = pltpu.roll(partial[:, 2 * out_c :], width - 1, 0)
    left = jnp.where(at == 0, 0.0, left)
    right = jnp.where(at == width - 1, 0.0, right)
    return left + partial[:, out_c : 2 * out_c] + right


def kernel(
    n_space, volume, first, second, out,
    field, hidden, partials, w1, w2, local_sem, send_sem, recv_sem,
):
    s, c = lax.axis_index("space"), lax.axis_index("chan")
    other = 1 - c
    depth, planes, width, half = volume.shape
    out_c = first.shape[4]
    has_up, has_down = s < n_space - 1, s > 0
    up, down, across = {"space": s + 1}, {"space": s - 1}, {"chan": other}

    own_copy = pltpu.make_async_copy(
        volume, field.at[c, pl.ds(1, depth), pl.ds(1, planes)], local_sem.at[0]
    )
    own_copy.start()
    filter_copies = []
    for k, (src, dst) in enumerate(((first, w1), (second, w2))):
        for tap in range(3):
            filter_copies.append(
                pltpu.make_async_copy(
                    src.at[:, :, tap],
                    dst.at[:, :, :, pl.ds(tap * out_c, out_c)],
                    local_sem.at[1 + 3 * k + tap],
                )
            )
    for copy in filter_copies:
        copy.start()

    barrier = pltpu.get_barrier_semaphore()
    pl.semaphore_signal(barrier, inc=1, device_id=across, device_id_type=MESH)

    @pl.when(has_up)
    def _():
        pl.semaphore_signal(barrier, inc=1, device_id=up, device_id_type=MESH)

    @pl.when(has_down)
    def _():
        pl.semaphore_signal(barrier, inc=1, device_id=down, device_id_type=MESH)

    line = jnp.zeros((planes + 2, width, half), field.dtype)
    for buf in (field, hidden):
        for h in range(2):
            buf[h, 0] = line
            buf[h, depth + 1] = line

    @pl.when(jnp.logical_not(has_down))
    def _():
        for buf in (field, hidden):
            for h in range(2):
                buf[h, :, 0] = jnp.zeros((depth + 2, width, half), field.dtype)

    @pl.when(jnp.logical_not(has_up))
    def _():
        for buf in (field, hidden):
            for h in range(2):
                buf[h, :, planes + 1] = jnp.zeros((depth + 2, width, half), field.dtype)

    pl.semaphore_wait(barrier, 1 + has_up.astype(jnp.int32) + has_down.astype(jnp.int32))

    def remote(phase, kind, d):
        buf = field if phase == 0 else hidden
        which = other if kind in (FWD_UP, FWD_DOWN) else c
        if kind == CHAN:
            src, dst, dev = pl.ds(1, planes), pl.ds(1, planes), across
        elif kind in (OWN_UP, FWD_UP):
            src, dst, dev = pl.ds(planes, 1), pl.ds(0, 1), up
        else:
            src, dst, dev = pl.ds(1, 1), pl.ds(planes + 1, 1), down
        if phase == 0 and kind == CHAN:
            source = volume.at[d]
        elif phase == 0 and kind == OWN_UP:
            source = volume.at[d, pl.ds(planes - 1, 1)]
        elif phase == 0 and kind == OWN_DOWN:
            source = volume.at[d, pl.ds(0, 1)]
        else:
            source = buf.at[which, d + 1, src]
        return pltpu.make_async_remote_copy(
            src_ref=source,
            dst_ref=buf.at[which, d + 1, dst],
            send_sem=send_sem.at[phase, kind, d],
            recv_sem=recv_sem.at[phase, kind, d],
            device_id=dev,
            device_id_type=MESH,
        )

    def send_own(phase, d):
        remote(phase, CHAN, d).start()

        @pl.when(has_up)
        def _():
            remote(phase, OWN_UP, d).start()

        @pl.when(has_down)
        def _():
            remote(phase, OWN_DOWN, d).start()

    def forward(phase, d):
        remote(phase, CHAN, d).wait_recv()

        @pl.when(has_up)
        def _():
            remote(phase, FWD_UP, d).start()

        @pl.when(has_down)
        def _():
            remote(phase, FWD_DOWN, d).start()

    def await_halo(phase, d):
        @pl.when(has_down)
        def _():
            remote(phase, OWN_UP, d).wait_recv()
            remote(phase, FWD_UP, d).wait_recv()

        @pl.when(has_up)
        def _():
            remote(phase, OWN_DOWN, d).wait_recv()
            remote(phase, FWD_DOWN, d).wait_recv()

    def dot_planes(buf, w, d, plane, taps):
        lhs = jnp.concatenate(
            [buf[h, d + a, plane + b] for a in range(3) for b in taps for h in range(2)], axis=1
        )
        rows = w[:, taps[0] : taps[-1] + 1].reshape(lhs.shape[1], 3 * out_c)
        return jnp.dot(lhs, rows, preferred_element_type=jnp.float32)

    def inner_part(buf, w, d):
        for p in range(planes):
            taps = [b for b in range(3) if 1 <= p + b <= planes]
            partials[d, p] = dot_planes(buf, w, d, p, taps)

    def outer_part(buf, w, d):
        totals = []
        for p in range(planes):
            total = partials[d, p]
            for b in range(3):
                if not 1 <= p + b <= planes:
                    total = total + dot_planes(buf, w, d, p, [b])
            totals.append(shifted_out(total, out_c))
        return totals

    def send_volume(d, carry):
        send_own(0, d)
        return carry

    lax.fori_loop(0, depth, send_volume, 0)
    own_copy.wait()
    for copy in filter_copies[:3]:
        copy.wait()

    def conv_phase(phase, lead, finish):
        buf, w = (field, w1) if phase == 0 else (hidden, w2)

        def step(t, carry):
            @pl.when(t < depth)
            def _():
                forward(phase, t)

            @pl.when(jnp.logical_and(t >= 1, t <= depth))
            def _():
                inner_part(buf, w, t - 1)

            @pl.when(jnp.logical_and(t >= lead - 1, t < lead - 1 + depth))
            def _():
                await_halo(phase, t - (lead - 1))

            @pl.when(t >= lead)
            def _():
                finish(t - lead)

            return carry

        lax.fori_loop(0, depth + lead, step, 0)

    def finish_hidden(d):
        for p, total in enumerate(outer_part(field, w1, d)):
            hidden[c, d + 1, p + 1] = jnp.maximum(total, 0.0).astype(hidden.dtype)
        send_own(1, d)

    def finish_out(d):
        for p, total in enumerate(outer_part(hidden, w2, d)):
            total = total + field[c, d + 1, p + 1].astype(jnp.float32)
            out[d, p] = jnp.maximum(total, 0.0).astype(out.dtype)

    conv_phase(0, LEADS[0], finish_hidden)
    for copy in filter_copies[3:]:
        copy.wait()
    conv_phase(1, LEADS[1], finish_out)

    def drain(d, carry):
        for phase in range(2):
            remote(phase, CHAN, d).wait_send()

            @pl.when(has_up)
            def _():
                remote(phase, OWN_UP, d).wait_send()
                remote(phase, FWD_UP, d).wait_send()

            @pl.when(has_down)
            def _():
                remote(phase, OWN_DOWN, d).wait_send()
                remote(phase, FWD_DOWN, d).wait_send()

        return carry

    lax.fori_loop(0, depth, drain, 0)


def per_device(n_space, volume, first_filter, second_filter):
    depth, planes, width, half = volume.shape
    taps_d, taps_h, taps_w, in_c, out_c = first_filter.shape
    plane_buf = pltpu.VMEM((2, depth + 2, planes + 2, width, half), jnp.bfloat16)
    filter_buf = pltpu.VMEM((taps_d, taps_h, in_c, taps_w * out_c), jnp.bfloat16)
    flops = 2 * 2 * 27 * depth * planes * width * in_c * out_c
    volume, first_filter, second_filter = (
        pltpu.with_memory_space_constraint(x, pltpu.HBM) for x in (volume, first_filter, second_filter)
    )
    return pl.pallas_call(
        functools.partial(kernel, n_space),
        out_shape=pltpu.VMEM(volume.shape, jnp.bfloat16),
        in_specs=[pl.BlockSpec(memory_space=pltpu.HBM)] * 3,
        out_specs=pl.BlockSpec(memory_space=pltpu.VMEM),
        scratch_shapes=[
            plane_buf,
            plane_buf,
            pltpu.VMEM((depth, planes, width, taps_w * out_c), jnp.float32),
            filter_buf,
            filter_buf,
            pltpu.SemaphoreType.DMA((7,)),
            pltpu.SemaphoreType.DMA((2, 5, depth)),
            pltpu.SemaphoreType.DMA((2, 5, depth)),
        ],
        compiler_params=pltpu.CompilerParams(
            collective_id=0, has_side_effects=True, vmem_limit_bytes=32 << 20
        ),
        cost_estimate=pl.CostEstimate(
            flops=flops, bytes_accessed=4 * volume.size + 4 * first_filter.size, transcendentals=0
        ),
    )(volume, first_filter, second_filter)


def solution(mesh):
    return jax.shard_map(
        functools.partial(per_device, mesh.shape["space"]),
        mesh=mesh,
        in_specs=(
            P(None, "space", None, "chan"),
            P(None, None, None, None, "chan"),
            P(None, None, None, None, "chan"),
        ),
        out_specs=P(None, "space", None, "chan"),
        check_vma=False,
    )
```

```python
import functools

import jax
import jax.numpy as jnp
from jax import lax
from jax.experimental import pallas as pl
from jax.experimental.pallas import tpu as pltpu
from jax.sharding import PartitionSpec as P

MESH = pl.DeviceIdType.MESH
LEADS = (4, 5)
CHAN, OWN_UP, OWN_DOWN, FWD_UP, FWD_DOWN = range(5)


def shifted_out(partial, out_c):
    width = partial.shape[0]
    at = lax.broadcasted_iota(jnp.int32, (width, out_c), 0)
    left = pltpu.roll(partial[:, :out_c], 1, 0)
    right = pltpu.roll(partial[:, 2 * out_c :], width - 1, 0)
    left = jnp.where(at == 0, 0.0, left)
    right = jnp.where(at == width - 1, 0.0, right)
    return left + partial[:, out_c : 2 * out_c] + right


def kernel(
    n_space, volume, first, second, out,
    field, hidden, partials, w1, w2, local_sem, send_sem, recv_sem,
):
    s, c = lax.axis_index("space"), lax.axis_index("chan")
    other = 1 - c
    depth, planes, width, half = volume.shape
    out_c = first.shape[4]
    has_up, has_down = s < n_space - 1, s > 0
    up, down, across = {"space": s + 1}, {"space": s - 1}, {"chan": other}

    barrier = pltpu.get_barrier_semaphore()
    pl.semaphore_signal(barrier, inc=1, device_id=across, device_id_type=MESH)

    @pl.when(has_up)
    def _():
        pl.semaphore_signal(barrier, inc=1, device_id=up, device_id_type=MESH)

    @pl.when(has_down)
    def _():
        pl.semaphore_signal(barrier, inc=1, device_id=down, device_id_type=MESH)

    line = jnp.zeros((planes + 2, width, half), field.dtype)
    for buf in (field, hidden):
        for h in range(2):
            buf[h, 0] = line
            buf[h, depth + 1] = line

    @pl.when(jnp.logical_not(has_down))
    def _():
        for buf in (field, hidden):
            for h in range(2):
                buf[h, :, 0] = jnp.zeros((depth + 2, width, half), field.dtype)

    @pl.when(jnp.logical_not(has_up))
    def _():
        for buf in (field, hidden):
            for h in range(2):
                buf[h, :, planes + 1] = jnp.zeros((depth + 2, width, half), field.dtype)

    pl.semaphore_wait(barrier, 1 + has_up.astype(jnp.int32) + has_down.astype(jnp.int32))

    def remote(phase, kind, d):
        buf = field if phase == 0 else hidden
        which = other if kind in (FWD_UP, FWD_DOWN) else c
        if kind == CHAN:
            src, dst, dev = pl.ds(1, planes), pl.ds(1, planes), across
        elif kind in (OWN_UP, FWD_UP):
            src, dst, dev = pl.ds(planes, 1), pl.ds(0, 1), up
        else:
            src, dst, dev = pl.ds(1, 1), pl.ds(planes + 1, 1), down
        if phase == 0 and kind == CHAN:
            source = volume.at[d]
        elif phase == 0 and kind == OWN_UP:
            source = volume.at[d, pl.ds(planes - 1, 1)]
        elif phase == 0 and kind == OWN_DOWN:
            source = volume.at[d, pl.ds(0, 1)]
        else:
            source = buf.at[which, d + 1, src]
        return pltpu.make_async_remote_copy(
            src_ref=source,
            dst_ref=buf.at[which, d + 1, dst],
            send_sem=send_sem.at[phase, kind, d],
            recv_sem=recv_sem.at[phase, kind, d],
            device_id=dev,
            device_id_type=MESH,
        )

    def send_own(phase, d):
        remote(phase, CHAN, d).start()

        @pl.when(has_up)
        def _():
            remote(phase, OWN_UP, d).start()

        @pl.when(has_down)
        def _():
            remote(phase, OWN_DOWN, d).start()

    def forward(phase, d):
        remote(phase, CHAN, d).wait_recv()

        @pl.when(has_up)
        def _():
            remote(phase, FWD_UP, d).start()

        @pl.when(has_down)
        def _():
            remote(phase, FWD_DOWN, d).start()

    def await_halo(phase, d):
        @pl.when(has_down)
        def _():
            remote(phase, OWN_UP, d).wait_recv()
            remote(phase, FWD_UP, d).wait_recv()

        @pl.when(has_up)
        def _():
            remote(phase, OWN_DOWN, d).wait_recv()
            remote(phase, FWD_DOWN, d).wait_recv()

    def dot_planes(buf, w, d, plane, taps):
        lhs = jnp.concatenate(
            [buf[h, d + a, plane + b] for a in range(3) for b in taps for h in range(2)], axis=1
        )
        rows = w[:, taps[0] : taps[-1] + 1].reshape(lhs.shape[1], 3 * out_c)
        return jnp.dot(lhs, rows, preferred_element_type=jnp.float32)

    def inner_part(buf, w, d):
        for p in range(planes):
            taps = [b for b in range(3) if 1 <= p + b <= planes]
            partials[d, p] = dot_planes(buf, w, d, p, taps)

    def outer_part(buf, w, d):
        totals = []
        for p in range(planes):
            total = partials[d, p]
            for b in range(3):
                if not 1 <= p + b <= planes:
                    total = total + dot_planes(buf, w, d, p, [b])
            totals.append(shifted_out(total, out_c))
        return totals

    def send_volume(d, carry):
        send_own(0, d)
        return carry

    lax.fori_loop(0, depth, send_volume, 0)

    own_copy = pltpu.make_async_copy(
        volume, field.at[c, pl.ds(1, depth), pl.ds(1, planes)], local_sem.at[0]
    )
    own_copy.start()
    filter_copies = []
    for k, (src, dst) in enumerate(((first, w1), (second, w2))):
        for tap in range(3):
            filter_copies.append(
                pltpu.make_async_copy(
                    src.at[:, :, tap],
                    dst.at[:, :, :, pl.ds(tap * out_c, out_c)],
                    local_sem.at[1 + 3 * k + tap],
                )
            )
    for copy in filter_copies:
        copy.start()

    own_copy.wait()
    for copy in filter_copies[:3]:
        copy.wait()

    def conv_phase(phase, lead, finish):
        buf, w = (field, w1) if phase == 0 else (hidden, w2)

        def step(t, carry):
            @pl.when(t < depth)
            def _():
                forward(phase, t)

            @pl.when(jnp.logical_and(t >= 1, t <= depth))
            def _():
                inner_part(buf, w, t - 1)

            @pl.when(jnp.logical_and(t >= lead - 1, t < lead - 1 + depth))
            def _():
                await_halo(phase, t - (lead - 1))

            @pl.when(t >= lead)
            def _():
                finish(t - lead)

            return carry

        lax.fori_loop(0, depth + lead, step, 0)

    def finish_hidden(d):
        for p, total in enumerate(outer_part(field, w1, d)):
            hidden[c, d + 1, p + 1] = jnp.maximum(total, 0.0).astype(hidden.dtype)
        send_own(1, d)

    def finish_out(d):
        for p, total in enumerate(outer_part(hidden, w2, d)):
            total = total + field[c, d + 1, p + 1].astype(jnp.float32)
            out[d, p] = jnp.maximum(total, 0.0).astype(out.dtype)

    conv_phase(0, LEADS[0], finish_hidden)
    for copy in filter_copies[3:]:
        copy.wait()
    conv_phase(1, LEADS[1], finish_out)

    def drain(d, carry):
        for phase in range(2):
            remote(phase, CHAN, d).wait_send()

            @pl.when(has_up)
            def _():
                remote(phase, OWN_UP, d).wait_send()
                remote(phase, FWD_UP, d).wait_send()

            @pl.when(has_down)
            def _():
                remote(phase, OWN_DOWN, d).wait_send()
                remote(phase, FWD_DOWN, d).wait_send()

        return carry

    lax.fori_loop(0, depth, drain, 0)


def per_device(n_space, volume, first_filter, second_filter):
    depth, planes, width, half = volume.shape
    taps_d, taps_h, taps_w, in_c, out_c = first_filter.shape
    plane_buf = pltpu.VMEM((2, depth + 2, planes + 2, width, half), jnp.bfloat16)
    filter_buf = pltpu.VMEM((taps_d, taps_h, in_c, taps_w * out_c), jnp.bfloat16)
    flops = 2 * 2 * 27 * depth * planes * width * in_c * out_c
    volume, first_filter, second_filter = (
        pltpu.with_memory_space_constraint(x, pltpu.HBM) for x in (volume, first_filter, second_filter)
    )
    return pl.pallas_call(
        functools.partial(kernel, n_space),
        out_shape=pltpu.VMEM(volume.shape, jnp.bfloat16),
        in_specs=[pl.BlockSpec(memory_space=pltpu.HBM)] * 3,
        out_specs=pl.BlockSpec(memory_space=pltpu.VMEM),
        scratch_shapes=[
            plane_buf,
            plane_buf,
            pltpu.VMEM((depth, planes, width, taps_w * out_c), jnp.float32),
            filter_buf,
            filter_buf,
            pltpu.SemaphoreType.DMA((7,)),
            pltpu.SemaphoreType.DMA((2, 5, depth)),
            pltpu.SemaphoreType.DMA((2, 5, depth)),
        ],
        compiler_params=pltpu.CompilerParams(
            collective_id=0, has_side_effects=True, vmem_limit_bytes=32 << 20
        ),
        cost_estimate=pl.CostEstimate(
            flops=flops, bytes_accessed=4 * volume.size + 4 * first_filter.size, transcendentals=0
        ),
    )(volume, first_filter, second_filter)


def solution(mesh):
    return jax.shard_map(
        functools.partial(per_device, mesh.shape["space"]),
        mesh=mesh,
        in_specs=(
            P(None, "space", None, "chan"),
            P(None, None, None, None, "chan"),
            P(None, None, None, None, "chan"),
        ),
        out_specs=P(None, "space", None, "chan"),
        check_vma=False,
    )
```

```python
import functools

import jax
import jax.numpy as jnp
from jax import lax
from jax.experimental import pallas as pl
from jax.experimental.pallas import tpu as pltpu
from jax.sharding import PartitionSpec as P

MESH = pl.DeviceIdType.MESH
LEADS = (4, 5)
CHAN, OWN_UP, OWN_DOWN, FWD_UP, FWD_DOWN = range(5)


def shifted_out(partial, out_c):
    width = partial.shape[0]
    at = lax.broadcasted_iota(jnp.int32, (width, out_c), 0)
    left = pltpu.roll(partial[:, :out_c], 1, 0)
    right = pltpu.roll(partial[:, 2 * out_c :], width - 1, 0)
    left = jnp.where(at == 0, 0.0, left)
    right = jnp.where(at == width - 1, 0.0, right)
    return left + partial[:, out_c : 2 * out_c] + right


def kernel(
    n_space, volume, first, second, out,
    field, hidden, partials, w1, w2, local_sem, send_sem, recv_sem,
):
    s, c = lax.axis_index("space"), lax.axis_index("chan")
    other = 1 - c
    depth, planes, width, half = volume.shape
    out_c = first.shape[4]
    has_up, has_down = s < n_space - 1, s > 0
    up, down, across = {"space": s + 1}, {"space": s - 1}, {"chan": other}

    own_copy = pltpu.make_async_copy(
        volume, field.at[c, pl.ds(1, depth), pl.ds(1, planes)], local_sem.at[0]
    )
    own_copy.start()
    filter_copies = []
    for k, (src, dst) in enumerate(((first, w1), (second, w2))):
        for tap in range(3):
            filter_copies.append(
                pltpu.make_async_copy(
                    src.at[:, :, tap],
                    dst.at[:, :, :, pl.ds(tap * out_c, out_c)],
                    local_sem.at[1 + 3 * k + tap],
                )
            )
    for copy in filter_copies:
        copy.start()

    barrier = pltpu.get_barrier_semaphore()
    pl.semaphore_signal(barrier, inc=1, device_id=across, device_id_type=MESH)

    @pl.when(has_up)
    def _():
        pl.semaphore_signal(barrier, inc=1, device_id=up, device_id_type=MESH)

    @pl.when(has_down)
    def _():
        pl.semaphore_signal(barrier, inc=1, device_id=down, device_id_type=MESH)

    line = jnp.zeros((planes + 2, width, half), field.dtype)
    for buf in (field, hidden):
        for h in range(2):
            buf[h, 0] = line
            buf[h, depth + 1] = line

    @pl.when(jnp.logical_not(has_down))
    def _():
        for buf in (field, hidden):
            for h in range(2):
                buf[h, :, 0] = jnp.zeros((depth + 2, width, half), field.dtype)

    @pl.when(jnp.logical_not(has_up))
    def _():
        for buf in (field, hidden):
            for h in range(2):
                buf[h, :, planes + 1] = jnp.zeros((depth + 2, width, half), field.dtype)

    pl.semaphore_wait(barrier, 1 + has_up.astype(jnp.int32) + has_down.astype(jnp.int32))

    def remote(phase, kind, d):
        buf = field if phase == 0 else hidden
        which = other if kind in (FWD_UP, FWD_DOWN) else c
        if kind == CHAN:
            src, dst, dev = pl.ds(1, planes), pl.ds(1, planes), across
        elif kind in (OWN_UP, FWD_UP):
            src, dst, dev = pl.ds(planes, 1), pl.ds(0, 1), up
        else:
            src, dst, dev = pl.ds(1, 1), pl.ds(planes + 1, 1), down
        if phase == 0 and kind == CHAN:
            source = volume.at[d]
        elif phase == 0 and kind == OWN_UP:
            source = volume.at[d, pl.ds(planes - 1, 1)]
        elif phase == 0 and kind == OWN_DOWN:
            source = volume.at[d, pl.ds(0, 1)]
        else:
            source = buf.at[which, d + 1, src]
        return pltpu.make_async_remote_copy(
            src_ref=source,
            dst_ref=buf.at[which, d + 1, dst],
            send_sem=send_sem.at[phase, kind, d],
            recv_sem=recv_sem.at[phase, kind, d],
            device_id=dev,
            device_id_type=MESH,
        )

    def send_own(phase, d):
        @pl.when(has_up)
        def _():
            remote(phase, OWN_UP, d).start()

        @pl.when(has_down)
        def _():
            remote(phase, OWN_DOWN, d).start()

        remote(phase, CHAN, d).start()

    def forward(phase, d):
        remote(phase, CHAN, d).wait_recv()

        @pl.when(has_up)
        def _():
            remote(phase, FWD_UP, d).start()

        @pl.when(has_down)
        def _():
            remote(phase, FWD_DOWN, d).start()

    def await_halo(phase, d):
        @pl.when(has_down)
        def _():
            remote(phase, OWN_UP, d).wait_recv()
            remote(phase, FWD_UP, d).wait_recv()

        @pl.when(has_up)
        def _():
            remote(phase, OWN_DOWN, d).wait_recv()
            remote(phase, FWD_DOWN, d).wait_recv()

    def dot_planes(buf, w, d, plane, taps):
        lhs = jnp.concatenate(
            [buf[h, d + a, plane + b] for a in range(3) for b in taps for h in range(2)], axis=1
        )
        rows = w[:, taps[0] : taps[-1] + 1].reshape(lhs.shape[1], 3 * out_c)
        return jnp.dot(lhs, rows, preferred_element_type=jnp.float32)

    def inner_part(buf, w, d):
        for p in range(planes):
            taps = [b for b in range(3) if 1 <= p + b <= planes]
            partials[d, p] = dot_planes(buf, w, d, p, taps)

    def outer_part(buf, w, d):
        totals = []
        for p in range(planes):
            total = partials[d, p]
            for b in range(3):
                if not 1 <= p + b <= planes:
                    total = total + dot_planes(buf, w, d, p, [b])
            totals.append(shifted_out(total, out_c))
        return totals

    def send_volume(d, carry):
        send_own(0, d)
        return carry

    lax.fori_loop(0, depth, send_volume, 0)
    own_copy.wait()
    for copy in filter_copies[:3]:
        copy.wait()

    def conv_phase(phase, lead, finish):
        buf, w = (field, w1) if phase == 0 else (hidden, w2)

        def step(t, carry):
            @pl.when(t < depth)
            def _():
                forward(phase, t)

            @pl.when(jnp.logical_and(t >= 1, t <= depth))
            def _():
                inner_part(buf, w, t - 1)

            @pl.when(jnp.logical_and(t >= lead - 1, t < lead - 1 + depth))
            def _():
                await_halo(phase, t - (lead - 1))

            @pl.when(t >= lead)
            def _():
                finish(t - lead)

            return carry

        lax.fori_loop(0, depth + lead, step, 0)

    def finish_hidden(d):
        for p, total in enumerate(outer_part(field, w1, d)):
            hidden[c, d + 1, p + 1] = jnp.maximum(total, 0.0).astype(hidden.dtype)
        send_own(1, d)

    def finish_out(d):
        for p, total in enumerate(outer_part(hidden, w2, d)):
            total = total + field[c, d + 1, p + 1].astype(jnp.float32)
            out[d, p] = jnp.maximum(total, 0.0).astype(out.dtype)

    conv_phase(0, LEADS[0], finish_hidden)
    for copy in filter_copies[3:]:
        copy.wait()
    conv_phase(1, LEADS[1], finish_out)

    def drain(d, carry):
        for phase in range(2):
            remote(phase, CHAN, d).wait_send()

            @pl.when(has_up)
            def _():
                remote(phase, OWN_UP, d).wait_send()
                remote(phase, FWD_UP, d).wait_send()

            @pl.when(has_down)
            def _():
                remote(phase, OWN_DOWN, d).wait_send()
                remote(phase, FWD_DOWN, d).wait_send()

        return carry

    lax.fori_loop(0, depth, drain, 0)


def per_device(n_space, volume, first_filter, second_filter):
    depth, planes, width, half = volume.shape
    taps_d, taps_h, taps_w, in_c, out_c = first_filter.shape
    plane_buf = pltpu.VMEM((2, depth + 2, planes + 2, width, half), jnp.bfloat16)
    filter_buf = pltpu.VMEM((taps_d, taps_h, in_c, taps_w * out_c), jnp.bfloat16)
    flops = 2 * 2 * 27 * depth * planes * width * in_c * out_c
    volume, first_filter, second_filter = (
        pltpu.with_memory_space_constraint(x, pltpu.HBM) for x in (volume, first_filter, second_filter)
    )
    return pl.pallas_call(
        functools.partial(kernel, n_space),
        out_shape=pltpu.VMEM(volume.shape, jnp.bfloat16),
        in_specs=[pl.BlockSpec(memory_space=pltpu.HBM)] * 3,
        out_specs=pl.BlockSpec(memory_space=pltpu.VMEM),
        scratch_shapes=[
            plane_buf,
            plane_buf,
            pltpu.VMEM((depth, planes, width, taps_w * out_c), jnp.float32),
            filter_buf,
            filter_buf,
            pltpu.SemaphoreType.DMA((7,)),
            pltpu.SemaphoreType.DMA((2, 5, depth)),
            pltpu.SemaphoreType.DMA((2, 5, depth)),
        ],
        compiler_params=pltpu.CompilerParams(
            collective_id=0, has_side_effects=True, vmem_limit_bytes=32 << 20
        ),
        cost_estimate=pl.CostEstimate(
            flops=flops, bytes_accessed=4 * volume.size + 4 * first_filter.size, transcendentals=0
        ),
    )(volume, first_filter, second_filter)


def solution(mesh):
    return jax.shard_map(
        functools.partial(per_device, mesh.shape["space"]),
        mesh=mesh,
        in_specs=(
            P(None, "space", None, "chan"),
            P(None, None, None, None, "chan"),
            P(None, None, None, None, "chan"),
        ),
        out_specs=P(None, "space", None, "chan"),
        check_vma=False,
    )
```
